32 devices in a mesh: clus: 8 (over y, x, core), lab: 4 (over z).
Axes of the slice: x: 2, y: 2, z: 4, core: 2. Of those that a mesh axis runs over, the one named last changes fastest.
Arguments:
- queries: bfloat16 [4096, 768], P(('clus', 'lab')), may hold values from -6 to 6
- visits: int32 [4096, 4], P(('clus', 'lab')), may hold values from 0 to 15, all different within a row; in each aligned block of 128 rows (0 to 127, 128 to 255, ...) at most 64 rows name the same one
- positives: int32 [4096, 4], P(('clus', 'lab')), may hold values from 0 to 4095
- weights: bfloat16 [16, 4096, 768], P('clus', 'lab'), may hold values from -0.21875 to 0.21875
- momentum: float32 [16, 4096, 768], P('clus', 'lab'), may hold values from -24 to 24
Outputs:
- query_grad: float32 [4096, 768], P(('clus', 'lab'))
- weights_new: bfloat16 [16, 4096, 768], P('clus', 'lab')
- momentum_new: float32 [16, 4096, 768], P('clus', 'lab')
The draws below stay inside these ranges and needn't reach their ends.
Inputs may be any that keep to these rules, and one draw needn't show every extreme that they name: `visits`: each query names 4 different clusters; among the 128 queries of one device at most 64 visit any one cluster.
All inputs are finite; a program needn't handle non-finite values.
Results may differ from the reference program's by a relative error of at most 0.006.
Values may be sent and summed in bfloat16 or wider, within the bound.
A program may use at most 128 MiB of HBM per device.

```python
import math
import jax
import jax.numpy as jnp
import numpy as np
from jax import lax

D = 768
VISITS = 4
Q_DEV = 128
NCLUS = 16
CSIZE = 4096
CAP = 64
QUERIES = 4096


def plant(array, key, least, top_value):
    longest = array.shape.index(max(array.shape))
    spots = []
    for shift in (0, 1):
        where = [jax.random.randint(jax.random.fold_in(key, axis), (), 0, length) for axis, length in enumerate(array.shape)]
        where[longest] = (where[longest] + shift) % array.shape[longest]
        spots.append(tuple(where))
    return array.at[spots[0]].set(least).at[spots[1]].set(top_value)


def level_of(stream_key, shape, cuts, smallest, largest):
    factor_of = 1.0
    for axis_at, shards_of in cuts:
        heights = jax.random.uniform(jax.random.fold_in(jax.random.fold_in(stream_key, 6), axis_at), (shards_of,), jnp.float32, smallest / len(cuts), largest / len(cuts))
        factor_of = factor_of * jnp.repeat(jnp.exp(heights), shape[axis_at] // shards_of).reshape((-1,) + (1,) * (len(shape) - 1 - axis_at))
    return factor_of


def deal_out(stream_key, own, number, rows, count, top, reach, skew):
    sequence = jax.random.permutation(stream_key, count)
    packed, ordinary = portions_of(count, rows * top, reach, skew, True), portions_of(count, rows * top, reach, skew, False)
    places = jnp.arange(count)

    def named(tallies, turn):
        used = int((tallies > 0).sum())
        fixed = max(1, used // 4)
        passed = fixed + (places - fixed + turn * (used - fixed)) % max(1, count - fixed)
        return jnp.zeros((count,), jnp.int32).at[sequence[jnp.where(places < fixed, places, passed)]].set(jnp.asarray(tallies, jnp.int32))

    tallies = jnp.where(number % 4 == 0, named(packed, number // 4), named(ordinary, number - number // 4 - 1))
    mixed = jax.random.permutation(jax.random.fold_in(own, 3), count)
    donor, taker = mixed[0:count // 2 * 2:2], mixed[1:count // 2 * 2:2]
    room = jnp.minimum(tallies[donor] - 1, reach - tallies[taker]) // 2
    room = jnp.where((donor == sequence[0]) | (taker == sequence[0]) | (tallies[taker] == 0), 0, jnp.maximum(room, 0))
    passed = jax.random.randint(jax.random.fold_in(own, 4), (count // 2,), 0, 1 << 20) % (room + 1)
    tallies = tallies.at[donor].add(-passed).at[taker].add(passed)
    labels = jnp.searchsorted(jnp.cumsum(tallies), jnp.arange(rows * top), side="right").astype(jnp.int32)
    listing = labels.reshape(top, rows).T
    listing = listing[jax.random.permutation(jax.random.fold_in(own, 1), rows)]
    turn = jax.random.randint(jax.random.fold_in(own, 2), (rows, 1), 0, top)
    return jnp.take_along_axis(listing, (jnp.arange(top)[None, :] + turn) % top, axis=1)


def portions_of(count, total, most, skew, full):
    weights = [(1 << 20) // math.isqrt(rank ** skew) + 1 for rank in range(1, count + 1)]
    largest = most if full else min(most, max(-(-total // count), total * weights[0] // sum(weights)))
    least = 1 if total - largest >= count - 1 else 0
    given, spare = [largest] + [least] * (count - 1), total - largest - least * (count - 1)
    while spare > 0:
        movable = [i for i in range(1, count) if given[i] < largest] or [i for i in range(1, count) if given[i] < most]
        pool, left = sum([weights[i] for i in movable]), spare
        for i in movable:
            extra = min(most - given[i], max(1, left * weights[i] // pool), spare)
            given[i] = given[i] + extra
            spare = spare - extra
    return np.array(given)


def bell_draw(rng, shape, width, bound, pieces=(), held_as=jnp.bfloat16):
    level = level_of(rng, shape, pieces, -0.22, 0.18) if pieces else 1.0
    result = jax.random.normal(rng, shape, jnp.float32) * width * level
    return jnp.minimum(jnp.maximum(result, -bound), bound).astype(held_as)


def setup_inputs(seed: int = 0) -> dict:
    arg_keys = jax.random.split(jax.random.key(seed), 6)
    queries = bell_draw(arg_keys[0], (QUERIES, D), 1.0, 6.0, ((0, 32),))
    visits_keys = jax.random.split(jax.random.fold_in(arg_keys[1], 1), QUERIES // Q_DEV)
    visits_turns = jax.random.permutation(jax.random.fold_in(arg_keys[1], 3), QUERIES // Q_DEV)
    visits = jax.vmap(lambda own, number: deal_out(jax.random.fold_in(arg_keys[1], 2), own, number, Q_DEV, NCLUS, VISITS, CAP, 2))(visits_keys, visits_turns).reshape((QUERIES, VISITS))
    positives = plant(jax.random.randint(arg_keys[2], (QUERIES, VISITS), 0, CSIZE), jax.random.fold_in(arg_keys[2], 1), 0, CSIZE - 1).astype(jnp.int32)
    weights = bell_draw(arg_keys[3], (NCLUS, CSIZE, D), D ** -0.5, 0.21875, ((0, 8), (1, 4)))
    momentum = bell_draw(arg_keys[4], (NCLUS, CSIZE, D), 4.0, 24.0, ((0, 8), (1, 4)), jnp.float32)
    return {"queries": queries, "visits": visits, "positives": positives, "weights": weights, "momentum": momentum}


momentum_decay = 0.9
step_rate = 0.002


def reference(queries, visits, positives, weights, momentum):
    ndevices = QUERIES // Q_DEV
    flat_visits = visits.reshape(ndevices, Q_DEV * VISITS)
    one_hot = (flat_visits[:, :, None] == jnp.arange(NCLUS, dtype=jnp.int32)[None, None, :]).astype(jnp.int32)
    before = jnp.cumsum(one_hot, axis=1) - one_hot
    ranks = jnp.sum(before * one_hot, axis=2)
    columns = jnp.arange(ndevices, dtype=jnp.int32)[:, None] * CAP + ranks
    visit_ids = jnp.arange(QUERIES * VISITS, dtype=jnp.int32).reshape(ndevices, Q_DEV * VISITS)
    table = jnp.full((NCLUS, ndevices * CAP), -1, jnp.int32)
    table = table.at[flat_visits.reshape(-1), columns.reshape(-1)].set(visit_ids.reshape(-1))
    flat_positives = positives.reshape(-1)
    label_ids = jnp.arange(CSIZE, dtype=jnp.int32)

    def per_cluster(carry, inputs):
        ids, cluster_weights = inputs
        live = ids >= 0
        safe_ids = jnp.where(live, ids, 0)
        query_ids = (safe_ids // VISITS).astype(jnp.int32)
        arrived = queries[query_ids].astype(jnp.float32)
        label_tag = flat_positives[safe_ids]
        labels32 = cluster_weights.astype(jnp.float32)
        logits = jnp.dot(arrived, labels32.T, precision=lax.Precision.HIGHEST)
        target = (label_tag[:, None] == label_ids[None, :]).astype(jnp.float32)
        grad = jnp.where(live[:, None], jax.nn.sigmoid(logits) - target, 0.0)
        grad_low = lax.optimization_barrier(grad.astype(jnp.bfloat16))
        grad32 = grad_low.astype(jnp.float32)
        query_part = jnp.dot(grad32, labels32, precision=lax.Precision.HIGHEST)
        carry = carry.at[query_ids].add(jnp.where(live[:, None], query_part, 0.0))
        label_grad = jnp.dot(grad32.T, arrived, precision=lax.Precision.HIGHEST)
        return carry, label_grad

    start = jnp.zeros((QUERIES, D), jnp.float32)
    query_grad, label_grad = lax.scan(per_cluster, start, (table, weights))
    momentum_new = momentum_decay * momentum + label_grad
    weights_new = (weights.astype(jnp.float32) - step_rate * momentum_new).astype(jnp.bfloat16)
    return (query_grad, weights_new, momentum_new)
```

```python
import functools

import jax
import jax.numpy as jnp
from jax import lax
from jax.experimental import pallas as pl
from jax.experimental.pallas import tpu as pltpu
from jax.sharding import PartitionSpec as P

momentum_decay = 0.9
step_rate = 0.002
BASE = 256
TAG_ROWS = 16
MESH = pl.DeviceIdType.MESH


def kernel(
    dims, blk_ref, w_hbm, m_hbm, out_ref, wn_hbm, mn_hbm,
    Q, A, G, R, RC, RD, RX, RY, RZ, W, M, PT, PS, TG, ssem, rsem, lsem, osem,
):
    n_lab, cap = dims
    planes = Q.shape[1]
    nz = Q.shape[2]
    q_count, width = R.shape[3:]
    clus_local, labels, _ = W.shape
    slots = clus_local * cap
    blocks = 2 * nz
    rows = blocks * cap
    f32, bf16 = jnp.float32, jnp.bfloat16

    clus, lab = lax.axis_index("clus"), lax.axis_index("lab")
    core = clus % 2
    sib = (clus + 1 - 2 * core, lab)
    xn = (clus + 2 - 4 * ((clus // 2) % 2), lab)
    yn = (clus + 4 - 8 * ((clus // 4) % 2), lab)
    zn = lambda d: (clus, (lab + d) % n_lab)

    def rc(src, dst, i, dev):
        return pltpu.make_async_remote_copy(
            src_ref=src, dst_ref=dst, send_sem=ssem.at[i], recv_sem=rsem.at[i],
            device_id=dev, device_id_type=MESH,
        )

    o = 0
    ag_z = {d: rc(Q.at[0, 0, 0], Q.at[0, 0, d], o + d - 1, zn(nz - d)) for d in range(1, nz)}
    o += nz - 1
    ag_x = [rc(Q.at[0, 0, d], Q.at[0, 1, d], o + d, xn) for d in range(nz)]
    o += nz
    ag_y = [rc(Q.at[0, 0, d], Q.at[0, 2, d], o + d, yn) for d in range(nz)]
    o += nz
    via_x = [d < nz // 2 for d in range(nz)]
    ag_d = [
        rc(Q.at[0, 1, d], Q.at[0, 3, d], o + d, yn)
        if via_x[d]
        else rc(Q.at[0, 2, d], Q.at[0, 3, d], o + d, xn)
        for d in range(nz)
    ]
    o += nz
    ag_s = [rc(Q.at[0, p], Q.at[1, p], o + p, sib) for p in range(planes)]
    o += planes
    rs_c = [rc(R.at[1, p], RC.at[p], o + p, sib) for p in range(planes)]
    o += planes
    rs_d = [rc(R.at[0, 3, d], RD.at[d], o + d, xn if via_x[d] else yn) for d in range(nz)]
    o += nz
    rs_x = [rc(R.at[0, 1, d], RX.at[d], o + d, xn) for d in range(nz)]
    o += nz
    rs_y = [rc(R.at[0, 2, d], RY.at[d], o + d, yn) for d in range(nz)]
    o += nz
    rs_z = {d: rc(R.at[0, 0, d], RZ.at[d - 1], o + d - 1, zn(d)) for d in range(1, nz)}

    own = pltpu.make_async_copy(blk_ref, Q.at[0, 0, 0], lsem.at[0])
    w_in = pltpu.make_async_copy(w_hbm, W, lsem.at[1])
    m_in = pltpu.make_async_copy(m_hbm, M, lsem.at[2])
    own.start()
    w_in.start()
    m_in.start()

    barrier = pltpu.get_barrier_semaphore()
    greet = [sib, xn, yn] + [zn(d) for d in range(1, nz)]
    for dev in greet:
        pl.semaphore_signal(barrier, inc=1, device_id=dev, device_id_type=MESH)
    pl.semaphore_wait(barrier, len(greet))

    own.wait()
    for d in range(1, nz):
        ag_z[d].start()
    ag_x[0].start()
    ag_y[0].start()
    for d in sorted(range(1, nz), key=lambda d: min(d, nz - d)):
        ag_z[d].wait_recv()
        ag_x[d].start()
        ag_y[d].start()
    ag_s[0].start()
    w_in.wait()

    iota_s = lax.broadcasted_iota(jnp.int32, (slots, q_count), 0).astype(f32)
    first = lax.broadcasted_iota(jnp.int32, (TAG_ROWS, q_count), 0)
    earlier = (
        lax.broadcasted_iota(jnp.int32, (q_count, q_count), 0)
        < lax.broadcasted_iota(jnp.int32, (q_count, q_count), 1)
    ).astype(f32).astype(bf16)
    base = (clus * clus_local).astype(f32)
    tile = 256

    def chunk(p):
        for b in range(blocks):
            c, d = b // nz, b % nz
            tags = Q[c, p, d, q_count:q_count + TAG_ROWS, 0:q_count].astype(f32)
            here, spot = [], []
            member = jnp.zeros((TAG_ROWS, q_count), f32)
            for j in range(clus_local):
                m = jnp.zeros((1, q_count), f32)
                pos = jnp.zeros((1, q_count), f32)
                for k in range(4):
                    hit = tags[k:k + 1] == base + j
                    m += jnp.where(hit, 1.0, 0.0)
                    pos += jnp.where(hit, tags[4 + k:5 + k] * BASE + tags[8 + k:9 + k] + 1.0, 0.0)
                here.append(m)
                spot.append(pos)
                member = jnp.where(first == j, jnp.broadcast_to(m, member.shape), member)
            rank = jnp.dot(member.astype(bf16), earlier, preferred_element_type=f32)
            pick = jnp.zeros((slots, q_count), f32)
            mark = jnp.zeros((slots, q_count), f32)
            for j in range(clus_local):
                goal = jnp.where(here[j] > 0.0, rank[j:j + 1] + float(j * cap), -1.0)
                same = iota_s == goal
                pick = jnp.where(same, 1.0, pick)
                mark = jnp.where(same, jnp.broadcast_to(spot[j], mark.shape), mark)
            pick = pick.astype(bf16)
            PT[b] = pick
            tag = jnp.sum(mark, axis=1, keepdims=True) - 1.0
            rowsq = jnp.dot(pick, Q[c, p, d, 0:q_count, :], preferred_element_type=f32).astype(bf16)
            for j in range(clus_local):
                A[j, p, b * cap:(b + 1) * cap, :] = rowsq[j * cap:(j + 1) * cap]
                TG[j, b * cap:(b + 1) * cap, :] = jnp.broadcast_to(
                    tag[j * cap:(j + 1) * cap], (cap, 128)
                )
        place = (lab * labels).astype(f32)

        @pl.loop(0, clus_local)
        def _(j):
            a = A[j, p]
            tag = TG[j][:, 0:1] - place
            for n in range(0, labels, tile):
                logits = lax.dot_general(
                    a, W[j, n:n + tile, :], (((1,), (1,)), ((), ())), preferred_element_type=f32
                )
                ids = lax.broadcasted_iota(jnp.int32, (rows, tile), 1).astype(f32) + float(n)
                g = 0.5 * jnp.tanh(0.5 * logits) + 0.5
                G[j, p, :, n:n + tile] = jnp.where(tag == ids, g - 1.0, g).astype(bf16)
            part = jnp.dot(G[j, p], W[j], preferred_element_type=f32).astype(bf16)
            PS[:, pl.ds(pl.multiple_of(j * cap, cap), cap), :] = part.reshape(blocks, cap, width)

        for b in range(blocks):
            R[b // nz, p, b % nz] = lax.dot_general(
                PT[b], PS[b], (((0,), (0,)), ((), ())), preferred_element_type=f32
            ).astype(bf16)

    def add_into(p, d, *others):
        s = R[0, p, d].astype(f32)
        for ref in others:
            s = s + ref.astype(f32)
        R[0, p, d] = s.astype(bf16)

    @pl.loop(0, planes)
    def _(p):
        @pl.when(p == 0)
        def _():
            ag_s[0].wait_recv()

        @pl.when(p == 1)
        def _():
            for d in range(nz):
                if via_x[d]:
                    ag_x[d].wait_recv()
                else:
                    ag_y[d].wait_recv()
                ag_d[d].start()
            for d in range(nz):
                if not via_x[d]:
                    ag_x[d].wait_recv()
            ag_s[1].start()
            for d in range(nz):
                if via_x[d]:
                    ag_y[d].wait_recv()
            ag_s[2].start()
            ag_s[1].wait_recv()

        @pl.when(p == 2)
        def _():
            for d in range(nz):
                ag_d[d].wait_recv()
            ag_s[3].start()
            ag_s[2].wait_recv()

        @pl.when(p == 3)
        def _():
            rs_c[1].wait_recv()
            for d in range(nz):
                add_into(1, d, RC[1, d])
                if via_x[d]:
                    rs_x[d].start()
            ag_s[3].wait_recv()

        chunk(p)
        for i in range(planes):
            @pl.when(p == i)
            def _(i=i):
                rs_c[i].start()

    rs_c[2].wait_recv()
    for d in range(nz):
        add_into(2, d, RC[2, d])
        if not via_x[d]:
            rs_y[d].start()
    rs_c[3].wait_recv()
    for d in range(nz):
        add_into(3, d, RC[3, d])
        rs_d[d].start()
    rs_c[0].wait_recv()
    for d in range(nz):
        add_into(0, d, RC[0, d])
    m_in.wait()

    lt = 256
    per = labels // lt
    steps = clus_local * per

    def outs(i):
        j, n = i // per, pl.multiple_of((i % per) * lt, lt)
        where = (j, pl.ds(n, lt))
        return (
            pltpu.make_async_copy(M.at[where], mn_hbm.at[where], osem.at[0, i]),
            pltpu.make_async_copy(W.at[where], wn_hbm.at[where], osem.at[1, i]),
        )

    def update(lo, hi):
        @pl.loop(lo, hi)
        def _(i):
            j, n = i // per, pl.multiple_of((i % per) * lt, lt)
            g = G[j, :, :, pl.ds(n, lt)].reshape(planes * rows, lt)
            a = A[j].reshape(planes * rows, width)
            lg = lax.dot_general(g, a, (((0,), (0,)), ((), ())), preferred_element_type=f32)
            mn = momentum_decay * M[j, pl.ds(n, lt), :] + lg
            wn = W[j, pl.ds(n, lt), :].astype(f32) - step_rate * mn
            M[j, pl.ds(n, lt), :] = mn
            W[j, pl.ds(n, lt), :] = wn.astype(bf16)
            for cp in outs(i):
                cp.start()

    update(0, steps // 4)
    for d in range(nz):
        rs_d[d].wait_recv()
        if via_x[d]:
            add_into(2, d, RD[d])
            rs_y[d].start()
        else:
            add_into(1, d, RD[d])
            rs_x[d].start()
    update(steps // 4, steps * 3 // 4)
    for d in list(range(1, nz)) + [0]:
        rs_x[d].wait_recv()
        rs_y[d].wait_recv()
        if d:
            add_into(0, d, RX[d], RY[d])
            rs_z[d].start()
    update(steps * 3 // 4, steps)
    total = R[0, 0, 0].astype(f32) + RX[0].astype(f32) + RY[0].astype(f32)
    for d in range(1, nz):
        rs_z[d].wait_recv()
        total = total + RZ[d - 1].astype(f32)
    out_ref[...] = total

    for cp in (
        list(ag_z.values()) + ag_x + ag_y + ag_d + ag_s
        + rs_c + rs_d + rs_x + rs_y + list(rs_z.values())
    ):
        cp.wait_send()

    @pl.loop(0, steps)
    def _(i):
        for cp in outs(i):
            cp.wait()


def fused(queries, visits, positives, weights, momentum):
    n_clus, n_lab = lax.axis_size("clus"), lax.axis_size("lab")
    q_count, width = queries.shape
    visit_count = visits.shape[1]
    clus_local, labels, _ = weights.shape
    cap = 2 * q_count * visit_count // (clus_local * n_clus)
    planes = n_clus // 2
    slots = clus_local * cap
    bf16, f32 = jnp.bfloat16, jnp.float32
    vt, pt = visits.T, positives.T
    tags = jnp.concatenate([vt, pt // BASE, pt % BASE], axis=0).astype(bf16)
    tags = jnp.pad(tags, ((0, TAG_ROWS - tags.shape[0]), (0, width - q_count)))
    blk = jnp.concatenate([queries, tags], axis=0)
    rows = 2 * n_lab * cap
    n_sem = 2 * (2 * (n_lab - 1) // 2) + 6 * n_lab + 2 * planes
    blocks = lambda *lead: pltpu.VMEM(lead + (q_count, width), bf16)
    any_spec = pl.BlockSpec(memory_space=pl.ANY)
    steps = clus_local * (labels // 256)
    return pl.pallas_call(
        functools.partial(kernel, (n_lab, cap)),
        out_shape=(
            jax.ShapeDtypeStruct((q_count, width), f32),
            jax.ShapeDtypeStruct(weights.shape, bf16),
            jax.ShapeDtypeStruct(momentum.shape, f32),
        ),
        in_specs=[any_spec] * 3,
        out_specs=(pl.BlockSpec(memory_space=pltpu.VMEM), any_spec, any_spec),
        scratch_shapes=[
            pltpu.VMEM((2, planes, n_lab, q_count + TAG_ROWS, width), bf16),
            pltpu.VMEM((clus_local, planes, rows, width), bf16),
            pltpu.VMEM((clus_local, planes, rows, labels), bf16),
            blocks(2, planes, n_lab),
            blocks(planes, n_lab),
            blocks(n_lab),
            blocks(n_lab),
            blocks(n_lab),
            blocks(n_lab - 1),
            pltpu.VMEM(weights.shape, bf16),
            pltpu.VMEM(momentum.shape, f32),
            pltpu.VMEM((2 * n_lab, slots, q_count), bf16),
            pltpu.VMEM((2 * n_lab, slots, width), bf16),
            pltpu.VMEM((clus_local, rows, 128), f32),
            pltpu.SemaphoreType.DMA((n_sem,)),
            pltpu.SemaphoreType.DMA((n_sem,)),
            pltpu.SemaphoreType.DMA((3,)),
            pltpu.SemaphoreType.DMA((2, steps)),
        ],
        compiler_params=pltpu.CompilerParams(
            collective_id=0, has_side_effects=True, vmem_limit_bytes=63 * 1024 * 1024
        ),
    )(blk, weights, momentum)


def shards(queries, visits, positives, weights, momentum):
    n_clus = lax.axis_size("clus")
    q_count, width = queries.shape
    visit_count = visits.shape[1]
    clus_local, block_size, _ = weights.shape
    all_clusters = clus_local * n_clus
    capacity = 2 * q_count * visit_count // all_clusters
    flat_visits = visits.reshape(-1)
    one_hot = (flat_visits[:, None] == jnp.arange(all_clusters, dtype=jnp.int32)[None, :]).astype(
        jnp.int32
    )
    before = jnp.cumsum(one_hot, axis=0) - one_hot
    ranks = jnp.sum(before * one_hot, axis=1)
    slots = flat_visits * capacity + ranks
    repeated = jnp.repeat(queries, visit_count, axis=0)
    outbox = jnp.zeros((all_clusters * capacity, width), jnp.bfloat16).at[slots].set(repeated)
    outbox = outbox.reshape(all_clusters, capacity, width)
    out_tags = (
        jnp.full((all_clusters * capacity,), -1, jnp.int32).at[slots].set(positives.reshape(-1))
    )
    out_tags = out_tags.reshape(all_clusters, capacity)
    landed, landed_tags = (
        lax.all_to_all(outbox, "clus", split_axis=0, concat_axis=1, tiled=True),
        lax.all_to_all(out_tags, "clus", split_axis=0, concat_axis=1, tiled=True),
    )
    arrived, label_tag = (
        lax.all_gather(landed, "lab", axis=1, tiled=True),
        lax.all_gather(landed_tags, "lab", axis=1, tiled=True),
    )
    offsets = lax.axis_index("lab") * block_size + jnp.arange(block_size, dtype=jnp.int32)
    logits = jnp.einsum("crd,cbd->crb", arrived, weights, preferred_element_type=jnp.float32)
    target = (label_tag[:, :, None] == offsets[None, None, :]).astype(jnp.float32)
    live = label_tag >= 0
    grad = jnp.where(live[:, :, None], jax.nn.sigmoid(logits) - target, 0.0).astype(jnp.bfloat16)
    partial_grad = jnp.einsum("crb,cbd->crd", grad, weights, preferred_element_type=jnp.float32)
    label_grad = jnp.einsum("crb,crd->cbd", grad, arrived, preferred_element_type=jnp.float32)
    folded = lax.psum_scatter(
        partial_grad.astype(jnp.bfloat16), "lab", scatter_dimension=1, tiled=True
    ).astype(jnp.float32)
    homed = lax.all_to_all(
        folded.astype(jnp.bfloat16), "clus", split_axis=1, concat_axis=0, tiled=True
    ).astype(folded.dtype)
    homed = homed.reshape(all_clusters * capacity, width)
    query_grad = jnp.sum(homed[slots].reshape(q_count, visit_count, width), axis=1)
    momentum_new = momentum_decay * momentum + label_grad
    weights_new = (weights.astype(jnp.float32) - step_rate * momentum_new).astype(jnp.bfloat16)
    return (query_grad, weights_new, momentum_new)


def solution(mesh):
    in_specs = (
        P(("clus", "lab"), None),
        P(("clus", "lab"), None),
        P(("clus", "lab"), None),
        P("clus", "lab", None),
        P("clus", "lab", None),
    )
    out_specs = (P(("clus", "lab"), None), P("clus", "lab", None), P("clus", "lab", None))
    planes = mesh.shape["clus"] // 2
    step = fused if planes == 4 else shards
    return jax.shard_map(step, mesh=mesh, in_specs=in_specs, out_specs=out_specs, check_vma=False)
```

```python
import functools

import jax
import jax.numpy as jnp
from jax import lax
from jax.experimental import pallas as pl
from jax.experimental.pallas import tpu as pltpu
from jax.sharding import PartitionSpec as P

momentum_decay = 0.9
step_rate = 0.002
BASE = 256
TAG_ROWS = 16
MESH = pl.DeviceIdType.MESH


def kernel(
    dims, q_hbm, t_hbm, w_hbm, m_hbm, out_ref, wn_hbm, mn_hbm,
    Q, A, G, R, RC, RD, RX, RY, RZ, W, M, PT, PS, TG, ssem, rsem, lsem, osem,
):
    n_lab, cap = dims
    planes = Q.shape[1]
    nz = Q.shape[2]
    q_count, width = R.shape[3:]
    clus_local, labels, _ = W.shape
    slots = clus_local * cap
    blocks = 2 * nz
    rows = blocks * cap
    f32, bf16 = jnp.float32, jnp.bfloat16

    clus, lab = lax.axis_index("clus"), lax.axis_index("lab")
    core = clus % 2
    sib = (clus + 1 - 2 * core, lab)
    xn = (clus + 2 - 4 * ((clus // 2) % 2), lab)
    yn = (clus + 4 - 8 * ((clus // 4) % 2), lab)
    zn = lambda d: (clus, (lab + d) % n_lab)

    def rc(src, dst, i, dev):
        return pltpu.make_async_remote_copy(
            src_ref=src, dst_ref=dst, send_sem=ssem.at[i], recv_sem=rsem.at[i],
            device_id=dev, device_id_type=MESH,
        )

    o = 0
    ag_z = {d: rc(Q.at[0, 0, 0], Q.at[0, 0, d], o + d - 1, zn(nz - d)) for d in range(1, nz)}
    o += nz - 1
    ag_x = [rc(Q.at[0, 0, d], Q.at[0, 1, d], o + d, xn) for d in range(nz)]
    o += nz
    ag_y = [rc(Q.at[0, 0, d], Q.at[0, 2, d], o + d, yn) for d in range(nz)]
    o += nz
    via_x = [d < nz // 2 for d in range(nz)]
    ag_d = [
        rc(Q.at[0, 1, d], Q.at[0, 3, d], o + d, yn)
        if via_x[d]
        else rc(Q.at[0, 2, d], Q.at[0, 3, d], o + d, xn)
        for d in range(nz)
    ]
    o += nz
    ag_s = [rc(Q.at[0, p], Q.at[1, p], o + p, sib) for p in range(planes - 1)]
    o += planes - 1
    ag_f = [rc(Q.at[0, 3, d], Q.at[1, 3, d], o + d, sib) for d in range(nz)]
    o += nz
    rs_c = [rc(R.at[1, p], RC.at[p], o + p, sib) for p in range(planes - 1)]
    o += planes - 1
    rs_f = [rc(R.at[1, 3, d], RC.at[3, d], o + d, sib) for d in range(nz)]
    o += nz
    late = [d for d in (1, 2, 0) if d < nz] + list(range(3, nz))
    rs_d = [rc(R.at[0, 3, d], RD.at[d], o + d, xn if via_x[d] else yn) for d in range(nz)]
    o += nz
    rs_x = [rc(R.at[0, 1, d], RX.at[d], o + d, xn) for d in range(nz)]
    o += nz
    rs_y = [rc(R.at[0, 2, d], RY.at[d], o + d, yn) for d in range(nz)]
    o += nz
    rs_z = {d: rc(R.at[0, 0, d], RZ.at[d - 1], o + d - 1, zn(d)) for d in range(1, nz)}

    own = pltpu.make_async_copy(q_hbm, Q.at[0, 0, 0, pl.ds(0, q_count)], lsem.at[0])
    own_tags = pltpu.make_async_copy(t_hbm, Q.at[0, 0, 0, pl.ds(q_count, TAG_ROWS)], lsem.at[3])
    w_in = pltpu.make_async_copy(w_hbm, W, lsem.at[1])
    m_in = pltpu.make_async_copy(m_hbm, M, lsem.at[2])
    own.start()
    own_tags.start()
    w_in.start()
    m_in.start()

    barrier = pltpu.get_barrier_semaphore()
    greet = [sib, xn, yn] + [zn(d) for d in range(1, nz)]
    for dev in greet:
        pl.semaphore_signal(barrier, inc=1, device_id=dev, device_id_type=MESH)
    pl.semaphore_wait(barrier, len(greet))

    own.wait()
    own_tags.wait()
    near = sorted(range(1, nz), key=lambda d: min(d, nz - d))
    ag_x[0].start()
    ag_y[0].start()
    for d in near:
        ag_z[d].start()

    def turn(d):
        (ag_x if via_x[d] else ag_y)[d].wait_recv()
        ag_d[d].start()

    ag_z[near[0]].wait_recv()
    ag_x[near[0]].start()
    ag_y[near[0]].start()
    turn(0)
    for d in near[1:]:
        ag_z[d].wait_recv()
        ag_x[d].start()
        ag_y[d].start()
    ag_s[0].start()
    turn(near[0])
    w_in.wait()

    iota_s = lax.broadcasted_iota(jnp.int32, (slots, q_count), 0).astype(f32)
    first = lax.broadcasted_iota(jnp.int32, (TAG_ROWS, q_count), 0)
    earlier = (
        lax.broadcasted_iota(jnp.int32, (q_count, q_count), 0)
        < lax.broadcasted_iota(jnp.int32, (q_count, q_count), 1)
    ).astype(f32).astype(bf16)
    base = (clus * clus_local).astype(f32)
    tile = 256

    def chunk(p):
        for b in range(blocks):
            c, d = b // nz, b % nz
            tags = Q[c, p, d, q_count:q_count + TAG_ROWS, 0:q_count].astype(f32)
            here, spot = [], []
            member = jnp.zeros((TAG_ROWS, q_count), f32)
            for j in range(clus_local):
                m = jnp.zeros((1, q_count), f32)
                pos = jnp.zeros((1, q_count), f32)
                for k in range(4):
                    hit = tags[k:k + 1] == base + j
                    m += jnp.where(hit, 1.0, 0.0)
                    pos += jnp.where(hit, tags[4 + k:5 + k] * BASE + tags[8 + k:9 + k] + 1.0, 0.0)
                here.append(m)
                spot.append(pos)
                member = jnp.where(first == j, jnp.broadcast_to(m, member.shape), member)
            rank = jnp.dot(member.astype(bf16), earlier, preferred_element_type=f32)
            pick = jnp.zeros((slots, q_count), f32)
            mark = jnp.zeros((slots, q_count), f32)
            for j in range(clus_local):
                goal = jnp.where(here[j] > 0.0, rank[j:j + 1] + float(j * cap), -1.0)
                same = iota_s == goal
                pick = jnp.where(same, 1.0, pick)
                mark = jnp.where(same, jnp.broadcast_to(spot[j], mark.shape), mark)
            pick = pick.astype(bf16)
            PT[b] = pick
            tag = jnp.sum(mark, axis=1, keepdims=True) - 1.0
            rowsq = jnp.dot(pick, Q[c, p, d, 0:q_count, :], preferred_element_type=f32).astype(bf16)
            for j in range(clus_local):
                A[j, p, b * cap:(b + 1) * cap, :] = rowsq[j * cap:(j + 1) * cap]
                TG[j, b * cap:(b + 1) * cap, :] = jnp.broadcast_to(
                    tag[j * cap:(j + 1) * cap], (cap, 128)
                )
        place = (lab * labels).astype(f32)

        @pl.loop(0, clus_local)
        def _(j):
            a = A[j, p]
            tag = TG[j][:, 0:1] - place
            for n in range(0, labels, tile):
                logits = lax.dot_general(
                    a, W[j, n:n + tile, :], (((1,), (1,)), ((), ())), preferred_element_type=f32
                )
                ids = lax.broadcasted_iota(jnp.int32, (rows, tile), 1).astype(f32) + float(n)
                g = 0.5 * jnp.tanh(0.5 * logits) + 0.5
                G[j, p, :, n:n + tile] = jnp.where(tag == ids, g - 1.0, g).astype(bf16)
            part = jnp.dot(G[j, p], W[j], preferred_element_type=f32).astype(bf16)
            PS[:, pl.ds(pl.multiple_of(j * cap, cap), cap), :] = part.reshape(blocks, cap, width)

        for b in range(blocks):
            R[b // nz, p, b % nz] = lax.dot_general(
                PT[b], PS[b], (((0,), (0,)), ((), ())), preferred_element_type=f32
            ).astype(bf16)

    def add_into(p, d, *others):
        s = R[0, p, d].astype(f32)
        for ref in others:
            s = s + ref.astype(f32)
        R[0, p, d] = s.astype(bf16)

    @pl.loop(0, planes)
    def _(p):
        @pl.when(p == 0)
        def _():
            ag_s[0].wait_recv()

        @pl.when(p == 1)
        def _():
            for d in near[1:]:
                turn(d)
            for d in range(nz):
                if not via_x[d]:
                    ag_x[d].wait_recv()
            ag_s[1].start()
            for d in range(nz):
                if via_x[d]:
                    ag_y[d].wait_recv()
            ag_s[2].start()
            ag_s[1].wait_recv()

        @pl.when(p == 2)
        def _():
            for d in range(nz):
                ag_d[d].wait_recv()
                ag_f[d].start()
            ag_s[2].wait_recv()

        @pl.when(p == 3)
        def _():
            rs_c[1].wait_recv()
            for d in range(nz):
                add_into(1, d, RC[1, d])
                if via_x[d]:
                    rs_x[d].start()
            for d in range(nz):
                ag_f[d].wait_recv()

        chunk(p)
        for i in range(planes):
            @pl.when(p == i)
            def _(i=i):
                if i < 3:
                    rs_c[i].start()
                else:
                    for d in late:
                        rs_f[d].start()

    rs_c[2].wait_recv()
    for d in range(nz):
        add_into(2, d, RC[2, d])
        if not via_x[d]:
            rs_y[d].start()
    for d in late:
        rs_f[d].wait_recv()
        add_into(3, d, RC[3, d])
        rs_d[d].start()
    rs_c[0].wait_recv()
    for d in range(nz):
        add_into(0, d, RC[0, d])
    m_in.wait()

    lt = 256
    per = labels // lt
    steps = clus_local * per

    def outs(i):
        j, n = i // per, pl.multiple_of((i % per) * lt, lt)
        where = (j, pl.ds(n, lt))
        return (
            pltpu.make_async_copy(M.at[where], mn_hbm.at[where], osem.at[0, i]),
            pltpu.make_async_copy(W.at[where], wn_hbm.at[where], osem.at[1, i]),
        )

    def update(lo, hi):
        @pl.loop(lo, hi)
        def _(i):
            j, n = i // per, pl.multiple_of((i % per) * lt, lt)
            g = G[j, :, :, pl.ds(n, lt)].reshape(planes * rows, lt)
            a = A[j].reshape(planes * rows, width)
            lg = lax.dot_general(g, a, (((0,), (0,)), ((), ())), preferred_element_type=f32)
            mn = momentum_decay * M[j, pl.ds(n, lt), :] + lg
            wn = W[j, pl.ds(n, lt), :].astype(f32) - step_rate * mn
            M[j, pl.ds(n, lt), :] = mn
            W[j, pl.ds(n, lt), :] = wn.astype(bf16)
            for cp in outs(i):
                cp.start()

    update(0, steps // 4)
    for d in late:
        rs_d[d].wait_recv()
        if via_x[d]:
            add_into(2, d, RD[d])
            rs_y[d].start()
        else:
            add_into(1, d, RD[d])
            rs_x[d].start()
    update(steps // 4, steps * 5 // 8)
    for d in [d for d in late if d] + [0]:
        rs_x[d].wait_recv()
        rs_y[d].wait_recv()
        if d:
            add_into(0, d, RX[d], RY[d])
            rs_z[d].start()
    update(steps * 5 // 8, steps)
    total = R[0, 0, 0].astype(f32) + RX[0].astype(f32) + RY[0].astype(f32)
    for d in range(1, nz):
        rs_z[d].wait_recv()
        total = total + RZ[d - 1].astype(f32)
    out_ref[...] = total

    for cp in (
        list(ag_z.values()) + ag_x + ag_y + ag_d + ag_s + ag_f
        + rs_c + rs_f + rs_d + rs_x + rs_y + list(rs_z.values())
    ):
        cp.wait_send()

    @pl.loop(0, steps)
    def _(i):
        for cp in outs(i):
            cp.wait()


def fused(queries, visits, positives, weights, momentum):
    n_clus, n_lab = lax.axis_size("clus"), lax.axis_size("lab")
    q_count, width = queries.shape
    visit_count = visits.shape[1]
    clus_local, labels, _ = weights.shape
    cap = 2 * q_count * visit_count // (clus_local * n_clus)
    planes = n_clus // 2
    slots = clus_local * cap
    bf16, f32 = jnp.bfloat16, jnp.float32
    vt, pt = visits.T, positives.T
    tags = jnp.concatenate([vt, pt // BASE, pt % BASE], axis=0).astype(bf16)
    tags = jnp.pad(tags, ((0, TAG_ROWS - tags.shape[0]), (0, width - q_count)))
    rows = 2 * n_lab * cap
    n_sem = 2 * (2 * (n_lab - 1) // 2) + 8 * n_lab + 2 * (planes - 1)
    blocks = lambda *lead: pltpu.VMEM(lead + (q_count, width), bf16)
    any_spec = pl.BlockSpec(memory_space=pl.ANY)
    steps = clus_local * (labels // 256)
    return pl.pallas_call(
        functools.partial(kernel, (n_lab, cap)),
        out_shape=(
            jax.ShapeDtypeStruct((q_count, width), f32),
            jax.ShapeDtypeStruct(weights.shape, bf16),
            jax.ShapeDtypeStruct(momentum.shape, f32),
        ),
        in_specs=[any_spec] * 4,
        out_specs=(pl.BlockSpec(memory_space=pltpu.VMEM), any_spec, any_spec),
        scratch_shapes=[
            pltpu.VMEM((2, planes, n_lab, q_count + TAG_ROWS, width), bf16),
            pltpu.VMEM((clus_local, planes, rows, width), bf16),
            pltpu.VMEM((clus_local, planes, rows, labels), bf16),
            blocks(2, planes, n_lab),
            blocks(planes, n_lab),
            blocks(n_lab),
            blocks(n_lab),
            blocks(n_lab),
            blocks(n_lab - 1),
            pltpu.VMEM(weights.shape, bf16),
            pltpu.VMEM(momentum.shape, f32),
            pltpu.VMEM((2 * n_lab, slots, q_count), bf16),
            pltpu.VMEM((2 * n_lab, slots, width), bf16),
            pltpu.VMEM((clus_local, rows, 128), f32),
            pltpu.SemaphoreType.DMA((n_sem,)),
            pltpu.SemaphoreType.DMA((n_sem,)),
            pltpu.SemaphoreType.DMA((4,)),
            pltpu.SemaphoreType.DMA((2, steps)),
        ],
        compiler_params=pltpu.CompilerParams(
            collective_id=0, has_side_effects=True, vmem_limit_bytes=63 * 1024 * 1024
        ),
    )(queries, tags, weights, momentum)


def shards(queries, visits, positives, weights, momentum):
    n_clus = lax.axis_size("clus")
    q_count, width = queries.shape
    visit_count = visits.shape[1]
    clus_local, block_size, _ = weights.shape
    all_clusters = clus_local * n_clus
    capacity = 2 * q_count * visit_count // all_clusters
    flat_visits = visits.reshape(-1)
    one_hot = (flat_visits[:, None] == jnp.arange(all_clusters, dtype=jnp.int32)[None, :]).astype(
        jnp.int32
    )
    before = jnp.cumsum(one_hot, axis=0) - one_hot
    ranks = jnp.sum(before * one_hot, axis=1)
    slots = flat_visits * capacity + ranks
    repeated = jnp.repeat(queries, visit_count, axis=0)
    outbox = jnp.zeros((all_clusters * capacity, width), jnp.bfloat16).at[slots].set(repeated)
    outbox = outbox.reshape(all_clusters, capacity, width)
    out_tags = (
        jnp.full((all_clusters * capacity,), -1, jnp.int32).at[slots].set(positives.reshape(-1))
    )
    out_tags = out_tags.reshape(all_clusters, capacity)
    landed, landed_tags = (
        lax.all_to_all(outbox, "clus", split_axis=0, concat_axis=1, tiled=True),
        lax.all_to_all(out_tags, "clus", split_axis=0, concat_axis=1, tiled=True),
    )
    arrived, label_tag = (
        lax.all_gather(landed, "lab", axis=1, tiled=True),
        lax.all_gather(landed_tags, "lab", axis=1, tiled=True),
    )
    offsets = lax.axis_index("lab") * block_size + jnp.arange(block_size, dtype=jnp.int32)
    logits = jnp.einsum("crd,cbd->crb", arrived, weights, preferred_element_type=jnp.float32)
    target = (label_tag[:, :, None] == offsets[None, None, :]).astype(jnp.float32)
    live = label_tag >= 0
    grad = jnp.where(live[:, :, None], jax.nn.sigmoid(logits) - target, 0.0).astype(jnp.bfloat16)
    partial_grad = jnp.einsum("crb,cbd->crd", grad, weights, preferred_element_type=jnp.float32)
    label_grad = jnp.einsum("crb,crd->cbd", grad, arrived, preferred_element_type=jnp.float32)
    folded = lax.psum_scatter(
        partial_grad.astype(jnp.bfloat16), "lab", scatter_dimension=1, tiled=True
    ).astype(jnp.float32)
    homed = lax.all_to_all(
        folded.astype(jnp.bfloat16), "clus", split_axis=1, concat_axis=0, tiled=True
    ).astype(folded.dtype)
    homed = homed.reshape(all_clusters * capacity, width)
    query_grad = jnp.sum(homed[slots].reshape(q_count, visit_count, width), axis=1)
    momentum_new = momentum_decay * momentum + label_grad
    weights_new = (weights.astype(jnp.float32) - step_rate * momentum_new).astype(jnp.bfloat16)
    return (query_grad, weights_new, momentum_new)


def solution(mesh):
    in_specs = (
        P(("clus", "lab"), None),
        P(("clus", "lab"), None),
        P(("clus", "lab"), None),
        P("clus", "lab", None),
        P("clus", "lab", None),
    )
    out_specs = (P(("clus", "lab"), None), P("clus", "lab", None), P("clus", "lab", None))
    planes = mesh.shape["clus"] // 2
    step = fused if planes == 4 else shards
    return jax.shard_map(step, mesh=mesh, in_specs=in_specs, out_specs=out_specs, check_vma=False)
```

```python
import functools

import jax
import jax.numpy as jnp
from jax import lax
from jax.experimental import pallas as pl
from jax.experimental.pallas import tpu as pltpu
from jax.sharding import PartitionSpec as P

momentum_decay = 0.9
step_rate = 0.002
BASE = 256
TAG_ROWS = 16
MESH = pl.DeviceIdType.MESH


def kernel(
    dims, q_hbm, t_hbm, w_hbm, m_hbm, out_ref, wn_hbm, mn_hbm,
    Q, A, G, R, RC, RD, RX, RY, RZ, W, M, PT, PS, TG, ssem, rsem, lsem, osem,
):
    n_lab, cap = dims
    planes = Q.shape[1]
    nz = Q.shape[2]
    q_count, width = R.shape[3:]
    clus_local, labels, _ = W.shape
    slots = clus_local * cap
    blocks = 2 * nz
    rows = blocks * cap
    f32, bf16 = jnp.float32, jnp.bfloat16

    clus, lab = lax.axis_index("clus"), lax.axis_index("lab")
    core = clus % 2
    sib = (clus + 1 - 2 * core, lab)
    xn = (clus + 2 - 4 * ((clus // 2) % 2), lab)
    yn = (clus + 4 - 8 * ((clus // 4) % 2), lab)
    zn = lambda d: (clus, (lab + d) % n_lab)

    def rc(src, dst, i, dev):
        return pltpu.make_async_remote_copy(
            src_ref=src, dst_ref=dst, send_sem=ssem.at[i], recv_sem=rsem.at[i],
            device_id=dev, device_id_type=MESH,
        )

    o = 0
    ag_z = {d: rc(Q.at[0, 0, 0], Q.at[0, 0, d], o + d - 1, zn(nz - d)) for d in range(1, nz)}
    o += nz - 1
    ag_x = [rc(Q.at[0, 0, d], Q.at[0, 1, d], o + d, xn) for d in range(nz)]
    o += nz
    ag_y = [rc(Q.at[0, 0, d], Q.at[0, 2, d], o + d, yn) for d in range(nz)]
    o += nz
    via_x = [d < nz // 2 for d in range(nz)]
    ag_d = [
        rc(Q.at[0, 1, d], Q.at[0, 3, d], o + d, yn)
        if via_x[d]
        else rc(Q.at[0, 2, d], Q.at[0, 3, d], o + d, xn)
        for d in range(nz)
    ]
    o += nz
    ag_s = [rc(Q.at[0, p], Q.at[1, p], o + p, sib) for p in range(planes - 1)]
    o += planes - 1
    ag_f = [rc(Q.at[0, 3, d], Q.at[1, 3, d], o + d, sib) for d in range(nz)]
    o += nz
    rs_c = [rc(R.at[1, p], RC.at[p], o + p, sib) for p in range(planes - 1)]
    o += planes - 1
    rs_f = [rc(R.at[1, 3, d], RC.at[3, d], o + d, sib) for d in range(nz)]
    o += nz
    late = [d for d in (1, 2, 0) if d < nz] + list(range(3, nz))
    rs_d = [rc(R.at[0, 3, d], RD.at[d], o + d, xn if via_x[d] else yn) for d in range(nz)]
    o += nz
    rs_x = [rc(R.at[0, 1, d], RX.at[d], o + d, xn) for d in range(nz)]
    o += nz
    rs_y = [rc(R.at[0, 2, d], RY.at[d], o + d, yn) for d in range(nz)]
    o += nz
    rs_z = {d: rc(R.at[0, 0, d], RZ.at[d - 1], o + d - 1, zn(d)) for d in range(1, nz)}

    own = pltpu.make_async_copy(q_hbm, Q.at[0, 0, 0, pl.ds(0, q_count)], lsem.at[0])
    own_tags = pltpu.make_async_copy(t_hbm, Q.at[0, 0, 0, pl.ds(q_count, TAG_ROWS)], lsem.at[3])
    w_in = pltpu.make_async_copy(w_hbm, W, lsem.at[1])
    m_in = pltpu.make_async_copy(m_hbm, M, lsem.at[2])
    own.start()
    own_tags.start()
    w_in.start()
    m_in.start()

    barrier = pltpu.get_barrier_semaphore()
    greet = [sib, xn, yn] + [zn(d) for d in range(1, nz)]
    for dev in greet:
        pl.semaphore_signal(barrier, inc=1, device_id=dev, device_id_type=MESH)
    pl.semaphore_wait(barrier, len(greet))

    own.wait()
    own_tags.wait()
    near = sorted(range(1, nz), key=lambda d: min(d, nz - d))
    ag_x[0].start()
    ag_y[0].start()
    for d in near:
        ag_z[d].start()

    def turn(d):
        (ag_x if via_x[d] else ag_y)[d].wait_recv()
        ag_d[d].start()

    ag_z[near[0]].wait_recv()
    ag_x[near[0]].start()
    ag_y[near[0]].start()
    turn(0)
    for d in near[1:]:
        ag_z[d].wait_recv()
        ag_x[d].start()
        ag_y[d].start()
    ag_s[0].start()
    turn(near[0])
    w_in.wait()

    iota_s = lax.broadcasted_iota(jnp.int32, (slots, q_count), 0).astype(f32)
    first = lax.broadcasted_iota(jnp.int32, (TAG_ROWS, q_count), 0)
    earlier = (
        lax.broadcasted_iota(jnp.int32, (q_count, q_count), 0)
        < lax.broadcasted_iota(jnp.int32, (q_count, q_count), 1)
    ).astype(f32).astype(bf16)
    base = (clus * clus_local).astype(f32)
    tile = 256

    def chunk(p):
        for b in range(blocks):
            c, d = b // nz, b % nz
            tags = Q[c, p, d, q_count:q_count + TAG_ROWS, 0:q_count].astype(f32)
            here, spot = [], []
            member = jnp.zeros((TAG_ROWS, q_count), f32)
            for j in range(clus_local):
                m = jnp.zeros((1, q_count), f32)
                pos = jnp.zeros((1, q_count), f32)
                for k in range(4):
                    hit = tags[k:k + 1] == base + j
                    m += jnp.where(hit, 1.0, 0.0)
                    pos += jnp.where(hit, tags[4 + k:5 + k] * BASE + tags[8 + k:9 + k] + 1.0, 0.0)
                here.append(m)
                spot.append(pos)
                member = jnp.where(first == j, jnp.broadcast_to(m, member.shape), member)
            rank = jnp.dot(member.astype(bf16), earlier, preferred_element_type=f32)
            pick = jnp.zeros((slots, q_count), f32)
            mark = jnp.zeros((slots, q_count), f32)
            for j in range(clus_local):
                goal = jnp.where(here[j] > 0.0, rank[j:j + 1] + float(j * cap), -1.0)
                same = iota_s == goal
                pick = jnp.where(same, 1.0, pick)
                mark = jnp.where(same, jnp.broadcast_to(spot[j], mark.shape), mark)
            pick = pick.astype(bf16)
            PT[b] = pick
            tag = jnp.sum(mark, axis=1, keepdims=True) - 1.0
            rowsq = jnp.dot(pick, Q[c, p, d, 0:q_count, :], preferred_element_type=f32).astype(bf16)
            for j in range(clus_local):
                A[j, p, b * cap:(b + 1) * cap, :] = rowsq[j * cap:(j + 1) * cap]
                TG[j, b * cap:(b + 1) * cap, :] = jnp.broadcast_to(
                    tag[j * cap:(j + 1) * cap], (cap, 128)
                )
        place = (lab * labels).astype(f32)

        @pl.loop(0, clus_local)
        def _(j):
            a = A[j, p]
            tag = TG[j][:, 0:1] - place
            for n in range(0, labels, tile):
                logits = lax.dot_general(
                    a, W[j, n:n + tile, :], (((1,), (1,)), ((), ())), preferred_element_type=f32
                )
                ids = lax.broadcasted_iota(jnp.int32, (rows, tile), 1).astype(f32) + float(n)
                g = 0.5 * jnp.tanh(0.5 * logits) + 0.5
                G[j, p, :, n:n + tile] = jnp.where(tag == ids, g - 1.0, g).astype(bf16)
            part = jnp.dot(G[j, p], W[j], preferred_element_type=f32).astype(bf16)
            PS[:, pl.ds(pl.multiple_of(j * cap, cap), cap), :] = part.reshape(blocks, cap, width)

        for b in range(blocks):
            R[b // nz, p, b % nz] = lax.dot_general(
                PT[b], PS[b], (((0,), (0,)), ((), ())), preferred_element_type=f32
            ).astype(bf16)

    def add_into(p, d, *others):
        s = R[0, p, d].astype(f32)
        for ref in others:
            s = s + ref.astype(f32)
        R[0, p, d] = s.astype(bf16)

    @pl.loop(0, planes)
    def _(p):
        @pl.when(p == 0)
        def _():
            ag_s[0].wait_recv()

        @pl.when(p == 1)
        def _():
            for d in near[1:]:
                turn(d)
            for d in range(nz):
                if not via_x[d]:
                    ag_x[d].wait_recv()
            ag_s[1].start()
            for d in range(nz):
                if via_x[d]:
                    ag_y[d].wait_recv()
            ag_s[2].start()
            ag_s[1].wait_recv()

        @pl.when(p == 2)
        def _():
            for d in range(nz):
                ag_d[d].wait_recv()
                ag_f[d].start()
            ag_s[2].wait_recv()

        @pl.when(p == 3)
        def _():
            rs_c[1].wait_recv()
            for d in range(nz):
                add_into(1, d, RC[1, d])
                if via_x[d]:
                    rs_x[d].start()
            rs_c[0].wait_recv()
            for d in range(nz):
                add_into(0, d, RC[0, d])
            rs_c[2].wait_recv()
            for d in range(nz):
                add_into(2, d, RC[2, d])
                if not via_x[d]:
                    rs_y[d].start()
            for d in range(nz):
                ag_f[d].wait_recv()

        chunk(p)
        for i in range(planes):
            @pl.when(p == i)
            def _(i=i):
                if i < 3:
                    rs_c[i].start()
                else:
                    for d in late:
                        rs_f[d].start()

    for d in late:
        rs_f[d].wait_recv()
        add_into(3, d, RC[3, d])
        rs_d[d].start()
    m_in.wait()

    lt = 256
    per = labels // lt
    steps = clus_local * per

    def outs(i):
        j, n = i // per, pl.multiple_of((i % per) * lt, lt)
        where = (j, pl.ds(n, lt))
        return (
            pltpu.make_async_copy(M.at[where], mn_hbm.at[where], osem.at[0, i]),
            pltpu.make_async_copy(W.at[where], wn_hbm.at[where], osem.at[1, i]),
        )

    def update(lo, hi):
        @pl.loop(lo, hi)
        def _(i):
            j, n = i // per, pl.multiple_of((i % per) * lt, lt)
            g = G[j, :, :, pl.ds(n, lt)].reshape(planes * rows, lt)
            a = A[j].reshape(planes * rows, width)
            lg = lax.dot_general(g, a, (((0,), (0,)), ((), ())), preferred_element_type=f32)
            mn = momentum_decay * M[j, pl.ds(n, lt), :] + lg
            wn = W[j, pl.ds(n, lt), :].astype(f32) - step_rate * mn
            M[j, pl.ds(n, lt), :] = mn
            W[j, pl.ds(n, lt), :] = wn.astype(bf16)
            for cp in outs(i):
                cp.start()

    update(0, steps // 4)
    for d in late:
        rs_d[d].wait_recv()
        if via_x[d]:
            add_into(2, d, RD[d])
            rs_y[d].start()
        else:
            add_into(1, d, RD[d])
            rs_x[d].start()
    update(steps // 4, steps * 5 // 8)
    for d in [d for d in late if d] + [0]:
        rs_x[d].wait_recv()
        rs_y[d].wait_recv()
        if d:
            add_into(0, d, RX[d], RY[d])
            rs_z[d].start()
    update(steps * 5 // 8, steps)
    total = R[0, 0, 0].astype(f32) + RX[0].astype(f32) + RY[0].astype(f32)
    for d in range(1, nz):
        rs_z[d].wait_recv()
        total = total + RZ[d - 1].astype(f32)
    out_ref[...] = total

    for cp in (
        list(ag_z.values()) + ag_x + ag_y + ag_d + ag_s + ag_f
        + rs_c + rs_f + rs_d + rs_x + rs_y + list(rs_z.values())
    ):
        cp.wait_send()

    @pl.loop(0, steps)
    def _(i):
        for cp in outs(i):
            cp.wait()


def fused(queries, visits, positives, weights, momentum):
    n_clus, n_lab = lax.axis_size("clus"), lax.axis_size("lab")
    q_count, width = queries.shape
    visit_count = visits.shape[1]
    clus_local, labels, _ = weights.shape
    cap = 2 * q_count * visit_count // (clus_local * n_clus)
    planes = n_clus // 2
    slots = clus_local * cap
    bf16, f32 = jnp.bfloat16, jnp.float32
    vt, pt = visits.T, positives.T
    tags = jnp.concatenate([vt, pt // BASE, pt % BASE], axis=0).astype(bf16)
    tags = jnp.pad(tags, ((0, TAG_ROWS - tags.shape[0]), (0, width - q_count)))
    rows = 2 * n_lab * cap
    n_sem = 2 * (2 * (n_lab - 1) // 2) + 8 * n_lab + 2 * (planes - 1)
    blocks = lambda *lead: pltpu.VMEM(lead + (q_count, width), bf16)
    any_spec = pl.BlockSpec(memory_space=pl.ANY)
    steps = clus_local * (labels // 256)
    return pl.pallas_call(
        functools.partial(kernel, (n_lab, cap)),
        out_shape=(
            jax.ShapeDtypeStruct((q_count, width), f32),
            jax.ShapeDtypeStruct(weights.shape, bf16),
            jax.ShapeDtypeStruct(momentum.shape, f32),
        ),
        in_specs=[any_spec] * 4,
        out_specs=(pl.BlockSpec(memory_space=pltpu.VMEM), any_spec, any_spec),
        scratch_shapes=[
            pltpu.VMEM((2, planes, n_lab, q_count + TAG_ROWS, width), bf16),
            pltpu.VMEM((clus_local, planes, rows, width), bf16),
            pltpu.VMEM((clus_local, planes, rows, labels), bf16),
            blocks(2, planes, n_lab),
            blocks(planes, n_lab),
            blocks(n_lab),
            blocks(n_lab),
            blocks(n_lab),
            blocks(n_lab - 1),
            pltpu.VMEM(weights.shape, bf16),
            pltpu.VMEM(momentum.shape, f32),
            pltpu.VMEM((2 * n_lab, slots, q_count), bf16),
            pltpu.VMEM((2 * n_lab, slots, width), bf16),
            pltpu.VMEM((clus_local, rows, 128), f32),
            pltpu.SemaphoreType.DMA((n_sem,)),
            pltpu.SemaphoreType.DMA((n_sem,)),
            pltpu.SemaphoreType.DMA((4,)),
            pltpu.SemaphoreType.DMA((2, steps)),
        ],
        compiler_params=pltpu.CompilerParams(
            collective_id=0, has_side_effects=True, vmem_limit_bytes=63 * 1024 * 1024
        ),
    )(queries, tags, weights, momentum)


def shards(queries, visits, positives, weights, momentum):
    n_clus = lax.axis_size("clus")
    q_count, width = queries.shape
    visit_count = visits.shape[1]
    clus_local, block_size, _ = weights.shape
    all_clusters = clus_local * n_clus
    capacity = 2 * q_count * visit_count // all_clusters
    flat_visits = visits.reshape(-1)
    one_hot = (flat_visits[:, None] == jnp.arange(all_clusters, dtype=jnp.int32)[None, :]).astype(
        jnp.int32
    )
    before = jnp.cumsum(one_hot, axis=0) - one_hot
    ranks = jnp.sum(before * one_hot, axis=1)
    slots = flat_visits * capacity + ranks
    repeated = jnp.repeat(queries, visit_count, axis=0)
    outbox = jnp.zeros((all_clusters * capacity, width), jnp.bfloat16).at[slots].set(repeated)
    outbox = outbox.reshape(all_clusters, capacity, width)
    out_tags = (
        jnp.full((all_clusters * capacity,), -1, jnp.int32).at[slots].set(positives.reshape(-1))
    )
    out_tags = out_tags.reshape(all_clusters, capacity)
    landed, landed_tags = (
        lax.all_to_all(outbox, "clus", split_axis=0, concat_axis=1, tiled=True),
        lax.all_to_all(out_tags, "clus", split_axis=0, concat_axis=1, tiled=True),
    )
    arrived, label_tag = (
        lax.all_gather(landed, "lab", axis=1, tiled=True),
        lax.all_gather(landed_tags, "lab", axis=1, tiled=True),
    )
    offsets = lax.axis_index("lab") * block_size + jnp.arange(block_size, dtype=jnp.int32)
    logits = jnp.einsum("crd,cbd->crb", arrived, weights, preferred_element_type=jnp.float32)
    target = (label_tag[:, :, None] == offsets[None, None, :]).astype(jnp.float32)
    live = label_tag >= 0
    grad = jnp.where(live[:, :, None], jax.nn.sigmoid(logits) - target, 0.0).astype(jnp.bfloat16)
    partial_grad = jnp.einsum("crb,cbd->crd", grad, weights, preferred_element_type=jnp.float32)
    label_grad = jnp.einsum("crb,crd->cbd", grad, arrived, preferred_element_type=jnp.float32)
    folded = lax.psum_scatter(
        partial_grad.astype(jnp.bfloat16), "lab", scatter_dimension=1, tiled=True
    ).astype(jnp.float32)
    homed = lax.all_to_all(
        folded.astype(jnp.bfloat16), "clus", split_axis=1, concat_axis=0, tiled=True
    ).astype(folded.dtype)
    homed = homed.reshape(all_clusters * capacity, width)
    query_grad = jnp.sum(homed[slots].reshape(q_count, visit_count, width), axis=1)
    momentum_new = momentum_decay * momentum + label_grad
    weights_new = (weights.astype(jnp.float32) - step_rate * momentum_new).astype(jnp.bfloat16)
    return (query_grad, weights_new, momentum_new)


def solution(mesh):
    in_specs = (
        P(("clus", "lab"), None),
        P(("clus", "lab"), None),
        P(("clus", "lab"), None),
        P("clus", "lab", None),
        P("clus", "lab", None),
    )
    out_specs = (P(("clus", "lab"), None), P("clus", "lab", None), P("clus", "lab", None))
    planes = mesh.shape["clus"] // 2
    step = fused if planes == 4 else shards
    return jax.shard_map(step, mesh=mesh, in_specs=in_specs, out_specs=out_specs, check_vma=False)
```
